32 devices in a mesh: wide: 8 (over y, x, core), narrow: 4 (over z).
Axes of the slice: x: 2, y: 2, z: 4, core: 2. Of those that a mesh axis runs over, the one named last changes fastest.
Arguments:
- inputs: bfloat16 [8, 2048, 1120], P('wide', 'narrow'), may hold values from -6 to 6
- cell_lengths: int32 [8, 32], P('wide'), may hold values from 1 to 512, 2048 in all within a row
- w_qkv: bfloat16 [1120, 3360], P('narrow'), may hold values from -0.1875 to 0.1875
- w_out: bfloat16 [1120, 1120], P('narrow'), may hold values from -0.5 to 0.5
- w_fc: bfloat16 [1120, 4480], P('narrow'), may hold values from -0.1875 to 0.1875
- w_proj: bfloat16 [4480, 1120], P('narrow'), may hold values from -0.09375 to 0.09375
- b_query: bfloat16 [1120], P('narrow'), may hold values from -3 to 3
- b_value: bfloat16 [1120], P('narrow'), may hold values from -3 to 3
- b_out: bfloat16 [1120], P('narrow'), may hold values from -3 to 3
- b_fc: bfloat16 [4480], P('narrow'), may hold values from -3 to 3
- b_proj: bfloat16 [1120], P('narrow'), may hold values from -3 to 3
- gain_attn: bfloat16 [1120], P('narrow'), may hold values from 0.25 to 1.75
- shift_attn: bfloat16 [1120], P('narrow'), may hold values from -3 to 3
- gain_mlp: bfloat16 [1120], P('narrow'), may hold values from 0.25 to 1.75
- shift_mlp: bfloat16 [1120], P('narrow'), may hold values from -3 to 3
- cotangent: bfloat16 [8, 2048, 1120], P('wide', 'narrow'), may hold values from -6 to 6
Outputs:
- outputs: bfloat16 [8, 2048, 1120], P('wide', 'narrow')
- d_inputs: float32 [8, 2048, 1120], P('wide', 'narrow')
- grad_wqkv: float32 [1120, 3360], P('narrow')
- grad_wout: float32 [1120, 1120], P('narrow')
- grad_wfc: float32 [1120, 4480], P('narrow')
- grad_wproj: float32 [4480, 1120], P('narrow')
- grad_bquery: float32 [1120], P('narrow')
- grad_bvalue: float32 [1120], P('narrow')
- grad_bout: float32 [1120], P('narrow')
- grad_bfc: float32 [4480], P('narrow')
- grad_bproj: float32 [1120], P('narrow')
- grad_gattn: float32 [1120], P('narrow')
- grad_sattn: float32 [1120], P('narrow')
- grad_gmlp: float32 [1120], P('narrow')
- grad_smlp: float32 [1120], P('narrow')
The draws below stay inside these ranges and needn't reach their ends.
Inputs may be any that keep to these rules, and one draw needn't show every extreme that they name: `cell_lengths`: each row's 32 cell lengths sum to 2048; every row's longest cell has exactly 512 positions.
All inputs are finite; a program needn't handle non-finite values.
Results may differ from the reference program's by a relative error of at most 0.012.
The reference program's roundings to bfloat16 on the way count: a program that leaves them out, or rounds other values in their place, can miss the bound.
Values may be sent and summed in bfloat16 or wider, within the bound.
No kernel may reach another device: no remote copies, remote signals or barrier semaphores. Data moves between devices by JAX's collectives and lax.ppermute only.
A program may use at most 320 MiB of HBM per device.

```python
import math
import jax
import jax.numpy as jnp
import numpy as np
from jax import lax

HEADS = 20
HEAD = 56
D = 1120
FF = 4480
ROW_LEN = 2048
CELLS = 32
SPAN = 512
ROWS = 8


def spiked(values, key, source, target, shards_of, factor):
    def block_of(dim):
        return (jnp.arange(values.shape[dim]) // (values.shape[dim] // shards_of)).reshape((-1,) + (1,) * (values.ndim - 1 - dim))

    first = jax.random.permutation(key, shards_of)[block_of(target)]
    other_side = (block_of(target) + shards_of // 2) % shards_of
    return jnp.where((block_of(source) == first) | (block_of(source) == other_side), factor * values, values)


def steps_of(rng, extent, shards, smallest, high):
    factor_of = 1.0
    for axis_at, parts in shards:
        draws = jax.random.uniform(jax.random.fold_in(jax.random.fold_in(rng, 6), axis_at), (parts,), jnp.float32, smallest / len(shards), high / len(shards))
        factor_of = factor_of * jnp.repeat(jnp.exp(draws), extent[axis_at] // parts).reshape((-1,) + (1,) * (len(extent) - 1 - axis_at))
    return factor_of


def split_up(number_of, total, bound, lean):
    weights = [(1 << 20) // math.isqrt(rank ** lean) + 1 for rank in range(2, number_of + 1)]
    surplus, holding = total - bound - (number_of - 1), [1] * (number_of - 1)
    while surplus > 0:
        movable = [i for i in range(number_of - 1) if holding[i] < bound]
        pool, left = sum([weights[i] for i in movable]), surplus
        for i in movable:
            addition = min(bound - holding[i], max(1, left * weights[i] // pool), surplus)
            holding[i] = holding[i] + addition
            surplus = surplus - addition
    return np.array([bound] + holding)


def uneven_parts(own_key, amount, total, limit, slope):
    if amount == 2:
        one = jax.random.randint(own_key, (), max(1, total - limit), min(limit, total - 1) + 1)
        return jnp.stack([one, total - one])
    sizes = jnp.asarray(split_up(amount, total, limit, slope), jnp.int32)
    pairs = (amount - 1) // 2
    giver, sink = sizes[1:1 + 2 * pairs:2], sizes[2:2 + 2 * pairs:2]
    slack = jnp.minimum(giver - 1, limit - sink)
    passed = jax.random.randint(jax.random.fold_in(own_key, 1), (pairs,), 0, 1 << 20) % (slack + 1)
    sizes = sizes.at[1:1 + 2 * pairs:2].set(giver - passed).at[2:2 + 2 * pairs:2].set(sink + passed)
    return sizes[jax.random.permutation(jax.random.fold_in(own_key, 2), amount)]


def scatter_about(stream_key, shape, scale, reach, pieces=(), kind=jnp.bfloat16):
    entries = jax.random.normal(stream_key, shape, jnp.float32) * scale
    if len(pieces) > 0:
        entries = steps_of(stream_key, shape, pieces, -0.22, 0.18) * entries
    return jnp.clip(entries, min=-reach, max=reach).astype(kind)


def heavy_noise(rng, dims, spread, bound, shards, heavy, kind=jnp.bfloat16):
    drawn = spread * jax.random.normal(rng, dims, jnp.float32)
    if shards:
        drawn = drawn * steps_of(rng, dims, shards, -0.22, 0.18)
    return jnp.clip(spiked(drawn, jax.random.fold_in(rng, 3), *heavy), -bound, bound).astype(kind)


def setup_inputs(seed: int = 0) -> dict:
    arg_keys = jax.random.split(jax.random.key(seed), 17)
    return {
        "inputs": scatter_about(arg_keys[0], (ROWS, ROW_LEN, D), 1.0, 6.0, ((0, 8), (1, 4))),
        "cell_lengths": jax.vmap(lambda own: uneven_parts(own, CELLS, ROW_LEN, SPAN, 1))(jax.random.split(arg_keys[1], ROWS)).reshape((ROWS, CELLS)).astype(jnp.int32),
        "w_qkv": scatter_about(arg_keys[2], (D, 3 * D), D ** -0.5, 0.1875, ((0, 4),)),
        "w_out": scatter_about(arg_keys[3], (D, D), (D // 8) ** -0.5, 0.5, ((0, 4),)),
        "w_fc": scatter_about(arg_keys[4], (D, FF), D ** -0.5, 0.1875, ((0, 4),)),
        "w_proj": scatter_about(arg_keys[5], (FF, D), FF ** -0.5, 0.09375, ((0, 4),)),
        "b_query": scatter_about(arg_keys[6], (D,), 0.5, 3.0, ((0, 4),)),
        "b_value": scatter_about(arg_keys[7], (D,), 0.5, 3.0, ((0, 4),)),
        "b_out": scatter_about(arg_keys[8], (D,), 0.5, 3.0, ((0, 4),)),
        "b_fc": scatter_about(arg_keys[9], (FF,), 0.5, 3.0, ((0, 4),)),
        "b_proj": scatter_about(arg_keys[10], (D,), 0.5, 3.0, ((0, 4),)),
        "gain_attn": jnp.clip(1.0 + 0.15 * jax.random.normal(arg_keys[11], (D,), jnp.float32), 0.25, 1.75).astype(jnp.bfloat16),
        "shift_attn": scatter_about(arg_keys[12], (D,), 0.5, 3.0, ((0, 4),)),
        "gain_mlp": jnp.clip(1.0 + 0.15 * jax.random.normal(arg_keys[13], (D,), jnp.float32), 0.25, 1.75).astype(jnp.bfloat16),
        "shift_mlp": scatter_about(arg_keys[14], (D,), 0.5, 3.0, ((0, 4),)),
        "cotangent": heavy_noise(arg_keys[15], (ROWS, ROW_LEN, D), 1.0, 6.0, ((0, 8), (1, 4)), (0, 2, 8, 2.0)),
    }


EPS = 1e-05

@jax.custom_vjp
def low(v):
    return lax.optimization_barrier(v.astype(jnp.bfloat16)).astype(jnp.float32)

@jax.custom_vjp
def low_back(v):
    return v

def low_keep(v):
    return (low(v), None)

def low_pass(kept, grad):
    return (grad,)

def back_keep(v):
    return (v, None)

def back_low(kept, grad):
    return (low(grad),)
low.defvjp(low_keep, low_pass)
low_back.defvjp(back_keep, back_low)

def rounded_both(values):
    return low_back(low(values))

def wide_dot(left, right):
    return jnp.dot(left, right, precision=lax.Precision.HIGHEST, preferred_element_type=jnp.float32)

def layer_norm(values, norm_gain, norm_shift):
    row_mean = lax.optimization_barrier(jnp.mean(values, axis=-1, keepdims=True))
    centered = values - row_mean
    row_var = lax.optimization_barrier(jnp.mean(centered * centered, axis=-1, keepdims=True))
    return centered * lax.rsqrt(row_var + EPS) * norm_gain + norm_shift

def attend(block):
    queries, key_rows, value_rows, query_ids, key_ids = block
    query_heads = queries.reshape(SPAN, HEADS, HEAD)
    key_heads = key_rows.reshape(2 * SPAN, HEADS, HEAD)
    value_heads = value_rows.reshape(2 * SPAN, HEADS, HEAD)
    scores = jnp.einsum('qhd,khd->hqk', query_heads, key_heads, precision=lax.Precision.HIGHEST) * HEAD ** (-0.5)
    scores = low_back(scores)
    causal = jnp.arange(2 * SPAN, dtype=jnp.int32)[None, :] <= jnp.arange(SPAN, dtype=jnp.int32)[:, None] + SPAN
    allowed = causal & (query_ids[:, None] == key_ids[None, :])
    masked = jnp.where(allowed[None], scores, -1e+30)
    row_max = lax.optimization_barrier(jnp.max(masked, axis=-1, keepdims=True))
    exponent = jnp.exp(masked - row_max)
    attn_probs = low(exponent / lax.optimization_barrier(jnp.sum(exponent, axis=-1, keepdims=True)))
    attn_mixed = jnp.einsum('hqk,khd->qhd', attn_probs, value_heads, precision=lax.Precision.HIGHEST)
    return attn_mixed.reshape(SPAN, HEADS * HEAD)

def windows(sequence, pad_value):
    group_size = sequence.shape[0]
    blocks_count = ROW_LEN // SPAN
    blocks = sequence.reshape((group_size, blocks_count, SPAN) + sequence.shape[2:])
    widths = [(0, 0), (1, 0), (0, 0)] + [(0, 0)] * (sequence.ndim - 2)
    earlier = jnp.pad(blocks, widths, constant_values=pad_value)[:, :-1]
    joined = jnp.concatenate([earlier, blocks], axis=2)
    return joined.reshape((group_size * blocks_count, 2 * SPAN) + sequence.shape[2:])

def forward(values_in, cell_ids, weights):
    w_qkv, w_out, w_fc, w_proj, b_query, b_value, b_out, b_fc, b_proj, gain_attn, shift_attn, gain_mlp, shift_mlp = weights
    group_size = values_in.shape[0]
    blocks_count = ROW_LEN // SPAN
    tokens = values_in.reshape(group_size * ROW_LEN, D)
    normed = low(layer_norm(tokens, gain_attn, shift_attn))
    projected = wide_dot(normed, w_qkv)
    queries = rounded_both(projected[:, :D] + b_query)
    key_rows = rounded_both(projected[:, D:2 * D])
    value_rows = rounded_both(projected[:, 2 * D:] + b_value)
    query_blocks = queries.reshape(group_size * blocks_count, SPAN, D)
    key_blocks = windows(key_rows.reshape(group_size, ROW_LEN, D), 0.0)
    value_blocks = windows(value_rows.reshape(group_size, ROW_LEN, D), 0.0)
    query_ids = cell_ids.reshape(group_size * blocks_count, SPAN)
    key_ids = windows(cell_ids, -1).astype(jnp.int32)
    attn_mixed = lax.map(jax.checkpoint(attend), (query_blocks, key_blocks, value_blocks, query_ids, key_ids))
    attn_mixed = rounded_both(attn_mixed.reshape(group_size * ROW_LEN, D))
    attn_branch = low_back(wide_dot(attn_mixed, w_out) + b_out)
    post_attention_state = tokens + attn_branch
    normed_mlp = low(layer_norm(post_attention_state, gain_mlp, shift_mlp))
    pre_act = low_back(wide_dot(normed_mlp, w_fc) + b_fc)
    hidden = low(jax.nn.gelu(pre_act, approximate=False))
    mlp_branch = low_back(wide_dot(hidden, w_proj) + b_proj)
    return (post_attention_state + mlp_branch).reshape(group_size, ROW_LEN, D)

def reference(inputs, cell_lengths, w_qkv, w_out, w_fc, w_proj, b_query, b_value, b_out, b_fc, b_proj, gain_attn, shift_attn, gain_mlp, shift_mlp, cotangent):
    params = tuple((p.astype(jnp.float32) for p in (w_qkv, w_out, w_fc, w_proj, b_query, b_value, b_out, b_fc, b_proj, gain_attn, shift_attn, gain_mlp, shift_mlp)))
    starts = (jnp.cumsum(cell_lengths, axis=-1) - cell_lengths).astype(jnp.int32)
    positions = jnp.arange(ROW_LEN, dtype=jnp.int32)
    cell_ids = (lax.optimization_barrier(jnp.sum((starts[:, None, :] <= positions[None, :, None]).astype(jnp.int32), axis=-1)) - 1).astype(jnp.int32)
    group_size = 2 if ROWS % 2 == 0 else 1
    group_count = ROWS // group_size
    input_groups = inputs.astype(jnp.float32).reshape(group_count, group_size, ROW_LEN, D)
    cot_groups = cotangent.astype(jnp.float32).reshape(group_count, group_size, ROW_LEN, D)
    id_groups = cell_ids.reshape(group_count, group_size, ROW_LEN)

    def group_step(running, item):
        group_rows, group_ids, group_cot = item

        def apply_layer(values_in, weights):
            return forward(values_in, group_ids, weights)
        result, pull_back = jax.vjp(apply_layer, group_rows, params)
        grad_rows, grad_params = pull_back(group_cot)
        summed = tuple((acc_term + new_term for acc_term, new_term in zip(running, grad_params)))
        return (summed, (result, grad_rows))
    initial = tuple((jnp.zeros_like(p) for p in params))
    totals, (results, grad_inputs) = lax.scan(group_step, initial, (input_groups, id_groups, cot_groups))
    return (results.reshape(ROWS, ROW_LEN, D).astype(jnp.bfloat16), grad_inputs.reshape(ROWS, ROW_LEN, D), totals[0], totals[1], totals[2], totals[3], totals[4], totals[5], totals[6], totals[7], totals[8], totals[9], totals[10], totals[11], totals[12])
```

```python
import functools

import jax
import jax.numpy as jnp
from jax import lax
from jax.experimental import pallas as pl
from jax.experimental.pallas import tpu as pltpu
from jax.sharding import PartitionSpec as P

HEADS = 20
HEAD = 56
EPS = 1e-05
BF = jnp.bfloat16
F32 = jnp.float32
ROOT_HALF = 0.7071067811865476
INV_ROOT_2PI = 0.3989422804014327
VMEM_LIMIT = 60 * 1024 * 1024


def params(n):
    return pltpu.CompilerParams(
        dimension_semantics=("arbitrary",) * n, vmem_limit_bytes=VMEM_LIMIT
    )


def mm(a, b):
    return jnp.dot(a, b, preferred_element_type=F32)


def mm_nt(a, b):
    return lax.dot_general(a, b, (((1,), (1,)), ((), ())), preferred_element_type=F32)


def mm_tn(a, b):
    return lax.dot_general(a, b, (((0,), (0,)), ((), ())), preferred_element_type=F32)


def standardize(values):
    mean = jnp.mean(values, axis=-1, keepdims=True)
    centered = values - mean
    var = jnp.mean(centered * centered, axis=-1, keepdims=True)
    inv = lax.rsqrt(var + EPS)
    return centered * inv, inv


def norm_pullback(grad, normed, inv, gain):
    scaled = grad * gain
    mean_grad = jnp.mean(scaled, axis=-1, keepdims=True)
    mean_proj = jnp.mean(scaled * normed, axis=-1, keepdims=True)
    return inv * (scaled - mean_grad - normed * mean_proj)


def head_window(h, width):
    low, high = h * HEAD, (h + 1) * HEAD
    a = low // 128 * 128
    b = min(-(-high // 128) * 128, width)
    lane = lax.broadcasted_iota(jnp.int32, (1, b - a), 1) + a
    return a, b, (lane >= low) & (lane < high)


def qkv_kernel(xp_ref, xo_ref, wq_ref, wk_ref, wv_ref, vec_ref, q_ref, k_ref, v_ref, nt_ref):
    step = pl.program_id(0)
    half = pl.num_programs(0) // 2
    x = jnp.where(step < half, xp_ref[...].astype(F32), xo_ref[...].astype(F32))
    normed, _ = standardize(x)
    n = (normed * vec_ref[0:1, :] + vec_ref[1:2, :]).astype(BF)
    k_ref[...] = mm(n, wk_ref[...]).astype(BF)
    v_ref[...] = (mm(n, wv_ref[...]) + vec_ref[3:4, :]).astype(BF)

    @pl.when(step >= half)
    def _():
        q_ref[...] = (mm(n, wq_ref[...]) + vec_ref[2:3, :]).astype(BF)
        nt_ref[...] = n.T


def ln_qkv(x_prev, x_own, wa, vec, tb):
    t, d = x_own.shape
    nb = t // tb
    own = lambda i: (jnp.maximum(i - nb, 0), 0)
    weight = lambda s: pl.BlockSpec((None, d, d), lambda i: (s, 0, 0))
    return pl.pallas_call(
        qkv_kernel,
        grid=(2 * nb,),
        in_specs=[
            pl.BlockSpec((tb, d), lambda i: (jnp.minimum(i, nb - 1), 0)),
            pl.BlockSpec((tb, d), own),
            weight(0),
            weight(1),
            weight(2),
            pl.BlockSpec(vec.shape, lambda i: (0, 0)),
        ],
        out_specs=[
            pl.BlockSpec((tb, d), own),
            pl.BlockSpec((tb, d), lambda i: (i, 0)),
            pl.BlockSpec((tb, d), lambda i: (i, 0)),
            pl.BlockSpec((d, tb), lambda i: (0, jnp.maximum(i - nb, 0))),
        ],
        out_shape=[
            jax.ShapeDtypeStruct((t, d), BF),
            jax.ShapeDtypeStruct((2 * t, d), BF),
            jax.ShapeDtypeStruct((2 * t, d), BF),
            jax.ShapeDtypeStruct((d, t), BF),
        ],
        compiler_params=params(1),
        name="ln_qkv",
    )(x_prev, x_own, wa, wa, wa, vec)


def attend_kernel(q_ref, k_ref, v_ref, qid_ref, kid_ref, o_ref, acc_ref):
    block, width = q_ref.shape
    band = kid_ref.shape[-1]
    base = pl.multiple_of(pl.program_id(0) * block, block)
    row = lax.broadcasted_iota(jnp.int32, (block, band), 0)
    col = lax.broadcasted_iota(jnp.int32, (block, band), 1)
    allowed = (qid_ref[...] == kid_ref[...]) & (col <= row + (band - block))
    bias = jnp.where(allowed, 0.0, -1e30)
    acc_ref[...] = jnp.zeros_like(acc_ref)
    for h in range(HEADS):
        a, b, lanes = head_window(h, width)
        query = jnp.where(lanes, q_ref[:, a:b].astype(F32), 0.0).astype(BF)
        scores = mm_nt(query, k_ref[pl.ds(base, band), a:b]) * HEAD**-0.5 + bias
        e = jnp.exp(scores - jnp.max(scores, axis=-1, keepdims=True))
        probs = (e / jnp.sum(e, axis=-1, keepdims=True)).astype(BF)
        out = mm(probs, v_ref[pl.ds(base, band), a:b])
        acc_ref[:, a:b] += jnp.where(lanes, out, 0.0)
    o_ref[...] = acc_ref[...].astype(BF)


def attend(q, k, v, qid, kid, block):
    t, d = q.shape
    band = kid.shape[-1]
    whole = pl.BlockSpec((2 * t, d), lambda i: (0, 0))
    return pl.pallas_call(
        attend_kernel,
        grid=(t // block,),
        in_specs=[
            pl.BlockSpec((block, d), lambda i: (i, 0)),
            whole,
            whole,
            pl.BlockSpec((block, 1), lambda i: (i, 0)),
            pl.BlockSpec((None, 1, band), lambda i: (i, 0, 0)),
        ],
        out_specs=pl.BlockSpec((block, d), lambda i: (i, 0)),
        out_shape=jax.ShapeDtypeStruct((t, d), BF),
        scratch_shapes=[pltpu.VMEM((block, d), F32)],
        compiler_params=params(1),
        name="attend",
    )(q, k, v, qid, kid)


def attend_back_kernel(
    q_ref, k_ref, v_ref, g_ref, qid_ref, kid_ref, dq_ref, prev_ref, own_ref, acc_ref, dk_ref, dv_ref
):
    step = pl.program_id(0)
    block, width = q_ref.shape
    band = kid_ref.shape[0]
    span = dk_ref.shape[0] // 2
    base = pl.multiple_of(step * block, block)
    keys = pl.ds(base, band)

    @pl.when(step == 0)
    def _():
        dk_ref[...] = jnp.zeros_like(dk_ref)
        dv_ref[...] = jnp.zeros_like(dv_ref)

    row = lax.broadcasted_iota(jnp.int32, (band, block), 0)
    col = lax.broadcasted_iota(jnp.int32, (band, block), 1)
    allowed = (qid_ref[...] == kid_ref[...]) & (row <= col + (band - block))
    bias = jnp.where(allowed, 0.0, -1e30)
    acc_ref[...] = jnp.zeros_like(acc_ref)
    scale = HEAD**-0.5
    for h in range(HEADS):
        a, b, lanes = head_window(h, width)
        query = jnp.where(lanes, q_ref[:, a:b].astype(F32), 0.0).astype(BF)
        grad = jnp.where(lanes, g_ref[:, a:b].astype(F32), 0.0).astype(BF)
        key = k_ref[keys, a:b]
        scores = mm_nt(key, query) * scale + bias
        e = jnp.exp(scores - jnp.max(scores, axis=0, keepdims=True))
        probs = e * (1.0 / jnp.sum(e, axis=0, keepdims=True))
        grad_probs = mm_nt(v_ref[keys, a:b], grad)
        dv_ref[keys, a:b] += mm(probs.astype(BF), grad)
        dot = jnp.sum(grad_probs * probs, axis=0, keepdims=True)
        grad_scores = (probs * (grad_probs - dot)).astype(BF)
        dk_ref[keys, a:b] += mm(grad_scores, query) * scale
        acc_ref[:, a:b] += jnp.where(lanes, mm_tn(grad_scores, key), 0.0)
    dq_ref[...] = (acc_ref[...] * scale).astype(BF)

    @pl.when(step == pl.num_programs(0) - 1)
    def _():
        prev_ref[0] = dk_ref[0:span, :].astype(BF)
        prev_ref[1] = dv_ref[0:span, :].astype(BF)
        own_ref[0] = dk_ref[span : 2 * span, :]
        own_ref[1] = dv_ref[span : 2 * span, :]


def attend_back(q, k, v, grad, qid, kid, block):
    t, d = q.shape
    band = kid.shape[1]
    whole = pl.BlockSpec((2 * t, d), lambda i: (0, 0))
    rows = pl.BlockSpec((block, d), lambda i: (i, 0))
    pair = pl.BlockSpec((2, t, d), lambda i: (0, 0, 0))
    return pl.pallas_call(
        attend_back_kernel,
        grid=(t // block,),
        in_specs=[
            rows,
            whole,
            whole,
            rows,
            pl.BlockSpec((1, block), lambda i: (0, i)),
            pl.BlockSpec((None, band, 1), lambda i: (i, 0, 0)),
        ],
        out_specs=[rows, pair, pair],
        out_shape=[
            jax.ShapeDtypeStruct((t, d), BF),
            jax.ShapeDtypeStruct((2, t, d), BF),
            jax.ShapeDtypeStruct((2, t, d), F32),
        ],
        scratch_shapes=[
            pltpu.VMEM((block, d), F32),
            pltpu.VMEM((2 * t, d), F32),
            pltpu.VMEM((2 * t, d), F32),
        ],
        compiler_params=params(1),
        name="attend_back",
    )(q, k, v, grad, qid, kid)


def mlp_kernel(
    x_ref, mixed_ref, cot_ref, wo_ref, wf_ref, wp_ref, vec_ref, bfc_ref,
    out_ref, ht_ref, gp_ref, nt_ref, mt_ref, ga_ref, gb_ref, gm_ref, gbfc_ref, sums_ref,
    after_ref, n_ref, oacc_ref, gacc_ref,
):
    chunk, tok = pl.program_id(0), pl.program_id(1)
    last = pl.num_programs(0) - 1
    tb = x_ref.shape[0]
    rows = pl.ds(pl.multiple_of(tok * tb, tb), tb)

    @pl.when(chunk == 0)
    def _():
        mixed = mixed_ref[...]
        after = x_ref[...].astype(F32) + (mm(mixed, wo_ref[...]) + vec_ref[0:1, :])
        normed, _ = standardize(after)
        n = (normed * vec_ref[1:2, :] + vec_ref[2:3, :]).astype(BF)
        after_ref[rows, :] = after
        n_ref[rows, :] = n
        mt_ref[...] = mixed.T
        nt_ref[...] = n.T
        oacc_ref[rows, :] = after + vec_ref[3:4, :]
        gacc_ref[rows, :] = jnp.zeros_like(after)

    @pl.when((chunk == 0) & (tok == 0))
    def _():
        sums_ref[...] = jnp.zeros_like(sums_ref)

    @pl.when(tok == 0)
    def _():
        gbfc_ref[...] = jnp.zeros_like(gbfc_ref)

    pre = mm(n_ref[rows, :], wf_ref[...]) + bfc_ref[...]
    phi = 0.5 + 0.5 * lax.erf(pre * ROOT_HALF)
    hidden = (pre * phi).astype(BF)
    slope = phi + pre * (jnp.exp(-0.5 * pre * pre) * INV_ROOT_2PI)
    cot = cot_ref[...]
    grad_pre = (mm_nt(cot, wp_ref[...]) * slope).astype(BF)
    oacc_ref[rows, :] += mm(hidden, wp_ref[...])
    gacc_ref[rows, :] += mm_nt(grad_pre, wf_ref[...])
    gp_ref[...] = grad_pre
    ht_ref[...] = hidden.T
    gbfc_ref[...] += jnp.sum(grad_pre.astype(F32), axis=0, keepdims=True)

    @pl.when(chunk == last)
    def _():
        out_ref[...] = oacc_ref[rows, :].astype(BF)
        normed, inv = standardize(after_ref[rows, :])
        grad_mid = gacc_ref[rows, :]
        wide_cot = cot.astype(F32)
        grad_after = wide_cot + norm_pullback(grad_mid, normed, inv, vec_ref[1:2, :])
        grad_attn = grad_after.astype(BF)
        ga_ref[...] = grad_after
        gb_ref[...] = grad_attn
        gm_ref[...] = mm_nt(grad_attn, wo_ref[...]).astype(BF)
        sums_ref[0:1, :] += jnp.sum(grad_mid * normed, axis=0, keepdims=True)
        sums_ref[1:2, :] += jnp.sum(grad_mid, axis=0, keepdims=True)
        sums_ref[2:3, :] += jnp.sum(grad_attn.astype(F32), axis=0, keepdims=True)
        sums_ref[3:4, :] += jnp.sum(wide_cot, axis=0, keepdims=True)


def mlp(x, mixed, cot, wa, wf, wp, vec, bfc, tb):
    t, d = x.shape
    nb, chunks = t // tb, wf.shape[0]
    first = lambda c, i: (jnp.where(c == 0, i, nb - 1), 0)
    first_t = lambda c, i: (0, jnp.where(c == 0, i, nb - 1))
    final = lambda c, i: (jnp.where(c == chunks - 1, i, 0), 0)
    rows = lambda index: pl.BlockSpec((tb, d), index)
    per_chunk = pl.BlockSpec((None, d, d), lambda c, i: (c, 0, 0))
    f32 = jax.ShapeDtypeStruct((t, d), F32)
    bf = jax.ShapeDtypeStruct((t, d), BF)
    bft = jax.ShapeDtypeStruct((d, t), BF)
    return pl.pallas_call(
        mlp_kernel,
        grid=(chunks, nb),
        in_specs=[
            rows(first),
            rows(first),
            rows(lambda c, i: (i, 0)),
            pl.BlockSpec((None, d, d), lambda c, i: (3, 0, 0)),
            per_chunk,
            per_chunk,
            pl.BlockSpec(vec.shape, lambda c, i: (0, 0)),
            pl.BlockSpec((None, 1, d), lambda c, i: (c, 0, 0)),
        ],
        out_specs=[
            rows(final),
            pl.BlockSpec((None, d, tb), lambda c, i: (c, 0, i)),
            pl.BlockSpec((None, tb, d), lambda c, i: (c, i, 0)),
            pl.BlockSpec((d, tb), first_t),
            pl.BlockSpec((d, tb), first_t),
            rows(final),
            rows(final),
            rows(final),
            pl.BlockSpec((None, 1, d), lambda c, i: (c, 0, 0)),
            pl.BlockSpec((8, d), lambda c, i: (0, 0)),
        ],
        out_shape=[
            bf,
            jax.ShapeDtypeStruct((chunks, d, t), BF),
            jax.ShapeDtypeStruct((chunks, t, d), BF),
            bft,
            bft,
            f32,
            bf,
            bf,
            jax.ShapeDtypeStruct((chunks, 1, d), F32),
            jax.ShapeDtypeStruct((8, d), F32),
        ],
        scratch_shapes=[
            pltpu.VMEM((t, d), F32),
            pltpu.VMEM((t, d), BF),
            pltpu.VMEM((t, d), F32),
            pltpu.VMEM((t, d), F32),
        ],
        compiler_params=params(2),
        name="mlp",
    )(x, mixed, cot, wa, wf, wp, vec, bfc)


def qkv_back_kernel(
    dq_ref, own_ref, next_ref, gb_ref, x_ref, ga_ref, wq_ref, wk_ref, wv_ref, vec_ref,
    dx_ref, gp_ref, sums_ref,
):
    @pl.when(pl.program_id(0) == 0)
    def _():
        sums_ref[...] = jnp.zeros_like(sums_ref)

    dq = dq_ref[...]
    dk = (own_ref[0] + next_ref[0].astype(F32)).astype(BF)
    dv = (own_ref[1] + next_ref[1].astype(F32)).astype(BF)
    gp_ref[0] = dq
    gp_ref[1] = dk
    gp_ref[2] = dv
    gp_ref[3] = gb_ref[...]
    grad = mm_nt(dq, wq_ref[...]) + mm_nt(dk, wk_ref[...]) + mm_nt(dv, wv_ref[...])
    normed, inv = standardize(x_ref[...].astype(F32))
    dx_ref[...] = ga_ref[...] + norm_pullback(grad, normed, inv, vec_ref[0:1, :])
    sums_ref[0:1, :] += jnp.sum(dq.astype(F32), axis=0, keepdims=True)
    sums_ref[1:2, :] += jnp.sum(dv.astype(F32), axis=0, keepdims=True)
    sums_ref[2:3, :] += jnp.sum(grad * normed, axis=0, keepdims=True)
    sums_ref[3:4, :] += jnp.sum(grad, axis=0, keepdims=True)


def qkv_back(dq, own, nxt, gb, x, ga, wa, vec, tb):
    t, d = x.shape
    rows = pl.BlockSpec((tb, d), lambda i: (i, 0))
    pair = pl.BlockSpec((2, tb, d), lambda i: (0, i, 0))
    weight = lambda s: pl.BlockSpec((None, d, d), lambda i: (s, 0, 0))
    return pl.pallas_call(
        qkv_back_kernel,
        grid=(t // tb,),
        in_specs=[
            rows, pair, pair, rows, rows, rows,
            weight(0), weight(1), weight(2),
            pl.BlockSpec(vec.shape, lambda i: (0, 0)),
        ],
        out_specs=[
            rows,
            pl.BlockSpec((4, tb, d), lambda i: (0, i, 0)),
            pl.BlockSpec((8, d), lambda i: (0, 0)),
        ],
        out_shape=[
            jax.ShapeDtypeStruct((t, d), F32),
            jax.ShapeDtypeStruct((4, t, d), BF),
            jax.ShapeDtypeStruct((8, d), F32),
        ],
        compiler_params=params(1),
        name="qkv_back",
    )(dq, own, nxt, gb, x, ga, wa, wa, wa, vec)


def weight_grad_kernel(place_ref, *refs):
    *pairs, out_ref = refs
    total = mm(pairs[0][...], pairs[1][...])
    for i in range(2, len(pairs), 2):
        total += mm(pairs[i][...], pairs[i + 1][...])
    out_ref[...] = total.astype(BF)


def weight_grad(pairs, left_of, right_of, place):
    m, t = pairs[0][0].shape[-2:]
    n = pairs[0][1].shape[-1]
    specs, operands = [], []
    for left, right in pairs:
        specs.append(pl.BlockSpec((None, m, t), lambda r, s: (left_of(r, r ^ s[0]), 0, 0)))
        specs.append(pl.BlockSpec((None, t, n), lambda r, s: (right_of(r, r ^ s[0]), 0, 0)))
        operands += [left, right]
    return pl.pallas_call(
        weight_grad_kernel,
        grid_spec=pltpu.PrefetchScalarGridSpec(
            num_scalar_prefetch=1,
            grid=(4,),
            in_specs=specs,
            out_specs=pl.BlockSpec((None, m, n), lambda r, s: (r, 0, 0)),
        ),
        out_shape=jax.ShapeDtypeStruct((4, m, n), BF),
        compiler_params=params(1),
        name="weight_grad",
    )(place, *operands)


def assemble_kernel(swapped, place_ref, own_ref, mine_ref, other_ref, out_ref, sems):
    chip, core, depth = place_ref[0], place_ref[1], place_ref[2]
    chunks, block, _ = own_ref.shape
    depths = mine_ref.shape[1] + 1
    piece = mine_ref.shape[2]
    skip = 2 * piece - block

    def target(chunk, z, start, size):
        row = pl.multiple_of((chunk if swapped else z) * block, 8) + start
        return out_ref.at[z if swapped else chunk, pl.ds(pl.multiple_of(row, 8), size), :]

    def run(halves):
        copies = []
        for r in range(chunks):
            chunk = r ^ chip
            copies.append((own_ref.at[chunk], target(chunk, depth, 0, block)))
            for d in range(1, depths):
                z = lax.rem(depth - d + depths, depths)
                copies.append(
                    (halves[0].at[r, d - 1], target(chunk, z, 0, piece))
                )
                copies.append(
                    (
                        halves[1].at[r, d - 1, pl.ds(skip, piece - skip), :],
                        target(chunk, z, piece, piece - skip),
                    )
                )
        started = [
            pltpu.make_async_copy(source, there, sems.at[i])
            for i, (source, there) in enumerate(copies)
        ]
        for copy in started:
            copy.start()
        for copy in started:
            copy.wait()

    @pl.when(core == 0)
    def _():
        run((mine_ref, other_ref))

    @pl.when(core == 1)
    def _():
        run((other_ref, mine_ref))


def assemble(own, mine, other, place, swapped):
    chunks, block, width = own.shape
    depths = mine.shape[1] + 1
    shape = (depths, chunks * block, width) if swapped else (chunks, depths * block, width)
    hbm = pl.BlockSpec(memory_space=pl.ANY)
    return pl.pallas_call(
        functools.partial(assemble_kernel, swapped),
        in_specs=[pl.BlockSpec(memory_space=pltpu.SMEM), hbm, hbm, hbm],
        out_specs=pl.BlockSpec(memory_space=pltpu.VMEM),
        out_shape=jax.ShapeDtypeStruct(shape, own.dtype),
        scratch_shapes=[pltpu.SemaphoreType.DMA((chunks * (2 * depths - 1),))],
        compiler_params=pltpu.CompilerParams(vmem_limit_bytes=VMEM_LIMIT),
        name="assemble",
    )(place, own, mine, other)


def flip(value, bit):
    count = lax.axis_size("wide")
    return lax.ppermute(value, "wide", [(i, i ^ bit) for i in range(count)])


def along(value, distance):
    count = lax.axis_size("narrow")
    return lax.ppermute(value, "narrow", [(i, (i + distance) % count) for i in range(count)])


def from_behind(value, distance):
    count = lax.axis_size("narrow")
    route = [(i - distance, i) for i in range(count) if 0 <= i - distance < count]
    return lax.ppermute(value, "narrow", route)


def add_low(*terms):
    total = terms[0].astype(F32)
    for term in terms[1:]:
        total = total + term.astype(F32)
    return total.astype(BF)


def plane_gather(value):
    half = value.shape[-2] // 2
    across_x = flip(value, 2)
    across_y = flip(value, 4)
    upper = flip(across_x[..., :half, :], 4)
    lower = flip(across_y[..., half:, :], 2)
    mine = jnp.stack([value, across_x, across_y, jnp.concatenate([upper, lower], axis=-2)])
    return mine, flip(mine, 1)


def plane_scatter(grads):
    half = grads.shape[-2] // 2
    upper = flip(grads[3][..., :half, :], 2)
    lower = flip(grads[3][..., half:, :], 4)
    to_x = jnp.concatenate(
        [grads[1][..., :half, :], add_low(grads[1][..., half:, :], lower)], axis=-2
    )
    to_y = jnp.concatenate(
        [add_low(grads[2][..., :half, :], upper), grads[2][..., half:, :]], axis=-2
    )
    return add_low(grads[0], flip(to_x, 2), flip(to_y, 4))


def depth_scatter(grads):
    parts = [grads[0]]
    for d in range(1, grads.shape[0]):
        parts.append(along(grads[d], d))
    return add_low(*parts)


def roll_from(value, start, axis):
    count = value.shape[axis]
    twice = jnp.concatenate([value, lax.slice_in_dim(value, 0, count - 1, axis=axis)], axis=axis)
    return lax.dynamic_slice_in_dim(twice, start, count, axis=axis)


def shards(
    inputs, cell_lengths, w_qkv, w_out, w_fc, w_proj, b_query, b_value, b_out, b_fc, b_proj,
    gain_attn, shift_attn, gain_mlp, shift_mlp, cotangent,
):
    _, span, d = inputs.shape
    depths = lax.axis_size("narrow")
    chips = lax.axis_size("wide") // 2
    block = w_qkv.shape[0]
    chunks = w_fc.shape[1] // d
    direct = chips == chunks == depths == 4 and block % 8 == 0
    wide_index = lax.axis_index("wide")
    chip, core = wide_index // 2, wide_index % 2
    depth = lax.axis_index("narrow")
    tb = min(256, span)
    qb = 128
    band = span + qb

    x_own = inputs.reshape(span, d)
    cot = cotangent.reshape(span, d)
    x_prev = from_behind(x_own, 1)

    own_a = jnp.stack([w_qkv[:, i * d : (i + 1) * d] for i in range(3)] + [w_out])
    own_f = jnp.stack([w_fc[:, i * d : (i + 1) * d] for i in range(chunks)])
    small = jnp.concatenate(
        [b_query, b_value, b_out, b_proj, gain_attn, shift_attn, gain_mlp, shift_mlp, b_fc]
    ).reshape(1, -1)
    if direct:
        piece = -(-block // 16) * 8
        place = jnp.stack([chip, core, depth]).astype(jnp.int32)
        own_p = w_proj.reshape(chunks, block, d)

        def gather(own, swapped):
            part = lax.dynamic_slice(own, (chip, core * (block - piece), 0), (1, piece, d))[0]
            foreign = jnp.stack([along(part, k) for k in range(1, depths)])
            mine, other = plane_gather(foreign)
            return assemble(own, mine, other, place, swapped)

        wa = gather(own_a, False)
        wf = gather(own_f, False)
        wp = gather(own_p, True)
        arrived = [small] + [along(small, k) for k in range(1, depths)]
        order = jnp.concatenate([arrived[(-e) % depths] for e in range(2 * depths)])
        small = lax.dynamic_slice_in_dim(order, (depths - depth) % depths, depths, axis=0)
    else:
        everything = lambda value, axis: lax.all_gather(value, "narrow", axis=axis, tiled=True)
        wa = everything(own_a, 1)
        wf = everything(own_f, 1)
        wp = everything(w_proj, 0).reshape(chunks, d, d)
        small = everything(small, 0)
    small = small.astype(F32)
    vectors = [small[:, i * block : (i + 1) * block].reshape(1, d) for i in range(8)]
    bias_q, bias_v, bias_o, bias_p, gain_1, shift_1, gain_2, shift_2 = vectors
    bias_f = small[:, 8 * block :].reshape(chunks, 1, d)
    vec_1 = jnp.concatenate([gain_1, shift_1, bias_q, bias_v] + [jnp.zeros_like(bias_q)] * 4)
    vec_2 = jnp.concatenate([bias_o, gain_2, shift_2, bias_p] + [jnp.zeros_like(bias_q)] * 4)

    starts = jnp.cumsum(cell_lengths, axis=-1) - cell_lengths
    pos = (depth - 1) * span + jnp.arange(2 * span, dtype=jnp.int32)
    ids = jnp.sum((starts <= pos[:, None]).astype(jnp.int32), axis=-1) - 1
    query_ids = ids[span:]
    key_ids = jnp.stack([ids[i * qb : i * qb + band] for i in range(span // qb)])

    q, k, v, nt_1 = ln_qkv(x_prev, x_own, wa, vec_1, tb)
    mixed = attend(q, k, v, query_ids[:, None], key_ids[:, None, :], qb)
    out, ht, gp_f, nt_2, mt, grad_after, grad_attn, grad_mixed, grad_bfc, sums_2 = mlp(
        x_own, mixed, cot, wa, wf, wp, vec_2, bias_f, tb
    )
    dq, kv_prev, kv_own = attend_back(
        q, k, v, grad_mixed, query_ids[None, :], key_ids[:, :, None], qb
    )
    kv_next = from_behind(kv_prev, -1)
    dx, gp_a, sums_1 = qkv_back(dq, kv_own, kv_next, grad_attn, x_own, grad_after, wa, vec_1, tb)

    left_a = jnp.stack([nt_1, mt])
    if direct:
        def halves(value):
            value = roll_from(value, depth, 1)
            take = lambda at: lax.dynamic_slice_in_dim(value, at * (block - piece), piece, axis=2)
            flat = lambda a: a.reshape(a.shape[0], depths * piece, span)
            return flat(take(core)), flip(flat(take(1 - core)), 1)

        def reduce(pairs, left_of, right_of):
            grads = weight_grad(pairs, left_of, right_of, place)
            grads = plane_scatter(grads.reshape(chunks, depths, piece, d))
            mine, other = plane_gather(depth_scatter(grads))
            first = jnp.where(core == 0, mine, other)
            second = jnp.where(core == 0, other, mine)[:, 2 * piece - block :, :]
            both = jnp.concatenate([first, second], axis=1)
            return [
                lax.dynamic_index_in_dim(both, i ^ chip, 0, keepdims=False).astype(F32)
                for i in range(chunks)
            ]

        by_chip = jnp.stack(
            [
                lax.dynamic_index_in_dim(
                    ht.reshape(depths, chunks, block, span), r ^ chip, 1, keepdims=False
                )
                for r in range(chunks)
            ]
        )
        here, there = halves(by_chip)
        cots = cot[None]
        shard_p = reduce(
            [(here, cots), (there, flip(cots, 1))], lambda r, c: r, lambda r, c: 0
        )
        here, there = halves(nt_2.reshape(1, depths, block, span))
        shard_f = reduce(
            [(here, gp_f), (there, flip(gp_f, 1))], lambda r, c: 0, lambda r, c: c
        )
        here, there = halves(left_a.reshape(2, depths, block, span))
        shard_a = reduce(
            [(here, gp_a), (there, flip(gp_a, 1))], lambda r, c: c // 3, lambda r, c: c
        )
        shard_p = jnp.concatenate(shard_p, axis=0)
    else:
        zero = jnp.zeros((1,), jnp.int32)

        def reduce(left, right, left_of, right_of, axis):
            grads = weight_grad([(left, right)], left_of, right_of, zero).astype(F32)
            grads = lax.psum(grads, "wide")
            return lax.psum_scatter(grads, "narrow", scatter_dimension=axis, tiled=True)

        shard_p = lax.psum(
            weight_grad([(ht, cot[None])], lambda r, c: c, lambda r, c: 0, zero).astype(F32), "wide"
        )
        shard_p = lax.psum_scatter(
            shard_p.reshape(chunks * d, d), "narrow", scatter_dimension=0, tiled=True
        )
        shard_f = reduce(nt_2[None], gp_f, lambda r, c: 0, lambda r, c: c, 1)
        shard_a = reduce(left_a, gp_a, lambda r, c: c // 3, lambda r, c: c, 1)
    shard_qkv = jnp.concatenate([shard_a[i] for i in range(3)], axis=1)
    shard_fc = jnp.concatenate([shard_f[i] for i in range(chunks)], axis=1)

    rows = [sums_1[0], sums_1[1], sums_2[2], sums_2[3], sums_1[2], sums_1[3], sums_2[0], sums_2[1]]
    packed = jnp.concatenate(
        [r.reshape(depths, block) for r in rows] + [grad_bfc.reshape(depths, chunks * block)], axis=1
    )
    packed = lax.psum(packed, ("wide", "narrow"))
    packed = lax.dynamic_index_in_dim(packed, depth, 0, keepdims=False)
    small_grads = [packed[i * block : (i + 1) * block] for i in range(8)]
    g_bq, g_bv, g_bo, g_bp, g_g1, g_s1, g_g2, g_s2 = small_grads
    return (
        out.reshape(inputs.shape),
        dx.reshape(inputs.shape),
        shard_qkv,
        shard_a[3],
        shard_fc,
        shard_p,
        g_bq,
        g_bv,
        g_bo,
        packed[8 * block :],
        g_bp,
        g_g1,
        g_s1,
        g_g2,
        g_s2,
    )


def solution(mesh):
    rows, flat = P("narrow", None), P("narrow")
    tokens = P("wide", "narrow", None)
    in_specs = (tokens, P("wide", None)) + (rows,) * 4 + (flat,) * 9 + (tokens,)
    out_specs = (tokens, tokens) + (rows,) * 4 + (flat,) * 9
    return jax.shard_map(shards, mesh=mesh, in_specs=in_specs, out_specs=out_specs, check_vma=False)
```

```python
import functools

import jax
import jax.numpy as jnp
from jax import lax
from jax.experimental import pallas as pl
from jax.experimental.pallas import tpu as pltpu
from jax.sharding import PartitionSpec as P

HEADS = 20
HEAD = 56
EPS = 1e-05
BF = jnp.bfloat16
F32 = jnp.float32
ROOT_HALF = 0.7071067811865476
INV_ROOT_2PI = 0.3989422804014327
LOG2_E = 1.4426950408889634
VMEM_LIMIT = 60 * 1024 * 1024


def params(n):
    return pltpu.CompilerParams(
        dimension_semantics=("arbitrary",) * n, vmem_limit_bytes=VMEM_LIMIT
    )


def mm(a, b):
    return jnp.dot(a, b, preferred_element_type=F32)


def mm_nt(a, b):
    return lax.dot_general(a, b, (((1,), (1,)), ((), ())), preferred_element_type=F32)


def mm_tn(a, b):
    return lax.dot_general(a, b, (((0,), (0,)), ((), ())), preferred_element_type=F32)


def standardize(values):
    mean = jnp.mean(values, axis=-1, keepdims=True)
    centered = values - mean
    var = jnp.mean(centered * centered, axis=-1, keepdims=True)
    inv = lax.rsqrt(var + EPS)
    return centered * inv, inv


def norm_pullback(grad, normed, inv, gain):
    scaled = grad * gain
    mean_grad = jnp.mean(scaled, axis=-1, keepdims=True)
    mean_proj = jnp.mean(scaled * normed, axis=-1, keepdims=True)
    return inv * (scaled - mean_grad - normed * mean_proj)


def lanes_of(width):
    return -(-width // 128) * 128


def padded(value, width):
    return jnp.concatenate(
        [value, jnp.zeros(value.shape[:-1] + (width - value.shape[-1],), value.dtype)], axis=-1
    )


def head_groups(lanes):
    groups = []
    for h in range(HEADS):
        if groups and (h + 1) * HEAD <= groups[-1][0] + 256:
            groups[-1][1].append(h)
        else:
            groups.append((min(h * HEAD // 128, lanes // 128 - 2) * 128, [h]))
    return groups


def own_lanes(start, h):
    lane = lax.broadcasted_iota(jnp.int32, (1, 256), 1) + start
    return (lane >= h * HEAD) & (lane < (h + 1) * HEAD)


def per_head(value, start, heads):
    wide = value.astype(F32)
    return jnp.concatenate(
        [jnp.where(own_lanes(start, h), wide, 0.0).astype(value.dtype) for h in heads], axis=0
    )


def joined(value, start, heads):
    rows = value.shape[0] // len(heads)
    total = None
    for i, h in enumerate(heads):
        term = jnp.where(own_lanes(start, h), value[i * rows : (i + 1) * rows], 0.0)
        total = term if total is None else total + term
    return total


def by_need(needed, band_blocks, run):
    widths = sorted({min(w, band_blocks) for w in (2, 3, band_blocks)})
    below = 0
    for w in widths:
        pl.when((needed > below) & (needed <= w))(functools.partial(run, w))
        below = w


def qkv_kernel(xp_ref, xo_ref, wq_ref, wk_ref, wv_ref, vec_ref, q_ref, k_ref, v_ref, nt_ref):
    step = pl.program_id(0)
    half = pl.num_programs(0) // 2
    x = jnp.where(step < half, xp_ref[...].astype(F32), xo_ref[...].astype(F32)).T
    normed, _ = standardize(x)
    n = (normed * vec_ref[0:1, :] + vec_ref[1:2, :]).astype(BF)
    lanes = k_ref.shape[1]
    k_ref[...] = padded(mm(n, wk_ref[...]).astype(BF), lanes)
    v_ref[...] = padded((mm(n, wv_ref[...]) + vec_ref[3:4, :]).astype(BF), lanes)

    @pl.when(step >= half)
    def _():
        q_ref[...] = padded((mm(n, wq_ref[...]) + vec_ref[2:3, :]).astype(BF), lanes)
        nt_ref[...] = n.T


def ln_qkv(x_prev, x_own, wa, vec, tb):
    d, t = x_own.shape
    nb = t // tb
    own = lambda i: (jnp.maximum(i - nb, 0), 0)
    weight = lambda s: pl.BlockSpec((None, d, d), lambda i: (s, 0, 0))
    return pl.pallas_call(
        qkv_kernel,
        grid=(2 * nb,),
        in_specs=[
            pl.BlockSpec((d, tb), lambda i: (0, jnp.minimum(i, nb - 1))),
            pl.BlockSpec((d, tb), lambda i: (0, jnp.maximum(i - nb, 0))),
            weight(0),
            weight(1),
            weight(2),
            pl.BlockSpec(vec.shape, lambda i: (0, 0)),
        ],
        out_specs=[
            pl.BlockSpec((tb, lanes_of(d)), own),
            pl.BlockSpec((tb, lanes_of(d)), lambda i: (i, 0)),
            pl.BlockSpec((tb, lanes_of(d)), lambda i: (i, 0)),
            pl.BlockSpec((d, tb), lambda i: (0, jnp.maximum(i - nb, 0))),
        ],
        out_shape=[
            jax.ShapeDtypeStruct((t, lanes_of(d)), BF),
            jax.ShapeDtypeStruct((2 * t, lanes_of(d)), BF),
            jax.ShapeDtypeStruct((2 * t, lanes_of(d)), BF),
            jax.ShapeDtypeStruct((d, t), BF),
        ],
        compiler_params=params(1),
        name="ln_qkv",
    )(x_prev, x_own, wa, wa, wa, vec)


def attend_kernel(need_ref, q_ref, k_ref, v_ref, qid_ref, kid_ref, o_ref, acc_ref):
    step = pl.program_id(0)
    block, lanes = q_ref.shape
    band = kid_ref.shape[-1]
    acc_ref[...] = jnp.zeros_like(acc_ref)

    def run(blocks):
        size = blocks * block
        keys = pl.ds(pl.multiple_of(step * block + band - size, block), size)
        row = lax.broadcasted_iota(jnp.int32, (block, size), 0)
        col = lax.broadcasted_iota(jnp.int32, (block, size), 1)
        allowed = (qid_ref[...] == kid_ref[:, band - size :]) & (col <= row + (size - block))
        bias = jnp.where(allowed, 0.0, -1e30)

        for start, heads in head_groups(lanes):
            window = slice(start, start + 256)
            query = per_head(q_ref[:, window], start, heads)
            scores = mm_nt(query, k_ref[keys, window]) * (HEAD**-0.5 * LOG2_E)
            scores += jnp.concatenate([bias] * len(heads), axis=0)
            e = jnp.exp2(scores - jnp.max(scores, axis=-1, keepdims=True))
            probs = (e * (1.0 / jnp.sum(e, axis=-1, keepdims=True))).astype(BF)
            acc_ref[:, window] += joined(mm(probs, v_ref[keys, window]), start, heads)

    by_need(need_ref[step], band // block, run)
    o_ref[...] = acc_ref[:, : o_ref.shape[1]].astype(BF)


def attend(need, q, k, v, qid, kid, block, d):
    t, lanes = q.shape
    band = kid.shape[-1]
    whole = pl.BlockSpec((2 * t, lanes), lambda i, s: (0, 0))
    return pl.pallas_call(
        attend_kernel,
        grid_spec=pltpu.PrefetchScalarGridSpec(
            num_scalar_prefetch=1,
            grid=(t // block,),
            in_specs=[
                pl.BlockSpec((block, lanes), lambda i, s: (i, 0)),
                whole,
                whole,
                pl.BlockSpec((block, 1), lambda i, s: (i, 0)),
                pl.BlockSpec((None, 1, band), lambda i, s: (i, 0, 0)),
            ],
            out_specs=pl.BlockSpec((block, d), lambda i, s: (i, 0)),
            scratch_shapes=[pltpu.VMEM((block, lanes), F32)],
        ),
        out_shape=jax.ShapeDtypeStruct((t, d), BF),
        compiler_params=params(1),
        name="attend",
    )(need, q, k, v, qid, kid)


def attend_back_kernel(
    need_ref, q_ref, k_ref, v_ref, g_ref, qid_ref, kid_ref,
    dq_ref, prev_ref, own_ref, acc_ref, dk_ref, dv_ref,
):
    step = pl.program_id(0)
    block, lanes = q_ref.shape
    width = dq_ref.shape[1]
    band = kid_ref.shape[0]
    span = dk_ref.shape[0] // 2
    scale = HEAD**-0.5

    @pl.when(step == 0)
    def _():
        dk_ref[...] = jnp.zeros_like(dk_ref)
        dv_ref[...] = jnp.zeros_like(dv_ref)

    acc_ref[...] = jnp.zeros_like(acc_ref)

    def run(blocks):
        size = blocks * block
        keys = pl.ds(pl.multiple_of(step * block + band - size, block), size)
        row = lax.broadcasted_iota(jnp.int32, (size, block), 0)
        col = lax.broadcasted_iota(jnp.int32, (size, block), 1)
        allowed = (qid_ref[...] == kid_ref[band - size :, :]) & (row <= col + (size - block))
        bias = jnp.where(allowed, 0.0, -1e30)

        for start, heads in head_groups(lanes):
            window = slice(start, start + 256)
            query = per_head(q_ref[:, window], start, heads)
            grad = per_head(g_ref[:, window], start, heads)
            key = k_ref[keys, window]
            scores = mm_nt(key, query) * (scale * LOG2_E)
            scores += jnp.concatenate([bias] * len(heads), axis=1)
            e = jnp.exp2(scores - jnp.max(scores, axis=0, keepdims=True))
            probs = e * (1.0 / jnp.sum(e, axis=0, keepdims=True))
            grad_probs = mm_nt(v_ref[keys, window], grad)
            dv_ref[keys, window] += mm(probs.astype(BF), grad)
            dot = jnp.sum(grad_probs * probs, axis=0, keepdims=True)
            grad_scores = (probs * (grad_probs - dot)).astype(BF)
            dk_ref[keys, window] += mm(grad_scores, query)
            acc_ref[:, window] += joined(mm_tn(grad_scores, key), start, heads)

    by_need(need_ref[step], band // block, run)
    dq_ref[...] = (acc_ref[:, :width] * scale).astype(BF)

    @pl.when(step == pl.num_programs(0) - 1)
    def _():
        prev_ref[0] = (dk_ref[0:span, :] * scale).astype(BF)
        prev_ref[1] = dv_ref[0:span, :].astype(BF)
        own_ref[0] = dk_ref[span : 2 * span, :width] * scale
        own_ref[1] = dv_ref[span : 2 * span, :width]


def attend_back(need, q, k, v, grad, qid, kid, block, d):
    t, lanes = q.shape
    band = kid.shape[1]
    whole = pl.BlockSpec((2 * t, lanes), lambda i, s: (0, 0))
    rows = pl.BlockSpec((block, lanes), lambda i, s: (i, 0))
    return pl.pallas_call(
        attend_back_kernel,
        grid_spec=pltpu.PrefetchScalarGridSpec(
            num_scalar_prefetch=1,
            grid=(t // block,),
            in_specs=[
                rows,
                whole,
                whole,
                rows,
                pl.BlockSpec((1, block), lambda i, s: (0, i)),
                pl.BlockSpec((None, band, 1), lambda i, s: (i, 0, 0)),
            ],
            out_specs=[
                pl.BlockSpec((block, d), lambda i, s: (i, 0)),
                pl.BlockSpec((2, t, lanes), lambda i, s: (0, 0, 0)),
                pl.BlockSpec((2, t, d), lambda i, s: (0, 0, 0)),
            ],
            scratch_shapes=[
                pltpu.VMEM((block, lanes), F32),
                pltpu.VMEM((2 * t, lanes), F32),
                pltpu.VMEM((2 * t, lanes), F32),
            ],
        ),
        out_shape=[
            jax.ShapeDtypeStruct((t, d), BF),
            jax.ShapeDtypeStruct((2, t, lanes), BF),
            jax.ShapeDtypeStruct((2, t, d), F32),
        ],
        compiler_params=params(1),
        name="attend_back",
    )(need, q, k, v, grad, qid, kid)


def mlp_kernel(
    x_ref, mixed_ref, cot_ref, wo_ref, wf_ref, wp_ref, vec_ref, bfc_ref,
    out_ref, ht_ref, gp_ref, nt_ref, mt_ref, ga_ref, gb_ref, gm_ref, gbfc_ref, sums_ref,
    after_ref, n_ref, oacc_ref, gacc_ref,
):
    chunk, tok = pl.program_id(0), pl.program_id(1)
    last = pl.num_programs(0) - 1
    tb, width = mixed_ref.shape
    rows = pl.ds(pl.multiple_of(tok * tb, tb), tb)

    @pl.when(chunk == 0)
    def _():
        mixed = mixed_ref[...]
        after = x_ref[...].astype(F32).T + (mm(mixed, wo_ref[...]) + vec_ref[0:1, :])
        normed, _ = standardize(after)
        n = (normed * vec_ref[1:2, :] + vec_ref[2:3, :]).astype(BF)
        after_ref[rows, :] = after
        n_ref[rows, :] = n
        mt_ref[...] = mixed.T
        nt_ref[...] = n.T
        oacc_ref[rows, :] = after + vec_ref[3:4, :]
        gacc_ref[rows, :] = jnp.zeros_like(after)

    @pl.when((chunk == 0) & (tok == 0))
    def _():
        sums_ref[...] = jnp.zeros_like(sums_ref)

    @pl.when(tok == 0)
    def _():
        gbfc_ref[...] = jnp.zeros_like(gbfc_ref)

    pre = mm(n_ref[rows, :], wf_ref[...]) + bfc_ref[...]
    phi = 0.5 + 0.5 * lax.erf(pre * ROOT_HALF)
    hidden = (pre * phi).astype(BF)
    slope = phi + pre * (jnp.exp(-0.5 * pre * pre) * INV_ROOT_2PI)
    cot = cot_ref[...].T
    grad_pre = (mm_nt(cot, wp_ref[...]) * slope).astype(BF)
    oacc_ref[rows, :] += mm(hidden, wp_ref[...])
    gacc_ref[rows, :] += mm_nt(grad_pre, wf_ref[...])
    gp_ref[:, :width] = grad_pre
    ht_ref[...] = hidden.T
    gbfc_ref[...] += jnp.sum(grad_pre.astype(F32), axis=0, keepdims=True)

    @pl.when(chunk == last)
    def _():
        out_ref[...] = oacc_ref[rows, :].astype(BF).T
        normed, inv = standardize(after_ref[rows, :])
        grad_mid = gacc_ref[rows, :]
        wide_cot = cot.astype(F32)
        grad_after = wide_cot + norm_pullback(grad_mid, normed, inv, vec_ref[1:2, :])
        grad_attn = grad_after.astype(BF)
        ga_ref[...] = grad_after
        gb_ref[...] = grad_attn
        gm_ref[...] = padded(mm_nt(grad_attn, wo_ref[...]).astype(BF), gm_ref.shape[1])
        sums_ref[0:1, :] += jnp.sum(grad_mid * normed, axis=0, keepdims=True)
        sums_ref[1:2, :] += jnp.sum(grad_mid, axis=0, keepdims=True)
        sums_ref[2:3, :] += jnp.sum(grad_attn.astype(F32), axis=0, keepdims=True)
        sums_ref[3:4, :] += jnp.sum(wide_cot, axis=0, keepdims=True)


def mlp(x, mixed, cot, wa, wf, wp, vec, bfc, tb):
    d, t = x.shape
    nb, chunks = t // tb, wf.shape[0]
    first = lambda c, i: (jnp.where(c == 0, i, nb - 1), 0)
    first_t = lambda c, i: (0, jnp.where(c == 0, i, nb - 1))
    final = lambda c, i: (jnp.where(c == chunks - 1, i, 0), 0)
    rows = lambda index: pl.BlockSpec((tb, d), index)
    per_chunk = pl.BlockSpec((None, d, d), lambda c, i: (c, 0, 0))
    f32 = jax.ShapeDtypeStruct((t, d), F32)
    bf = jax.ShapeDtypeStruct((t, d), BF)
    bft = jax.ShapeDtypeStruct((d, t), BF)
    return pl.pallas_call(
        mlp_kernel,
        grid=(chunks, nb),
        in_specs=[
            pl.BlockSpec((d, tb), first_t),
            rows(first),
            pl.BlockSpec((d, tb), lambda c, i: (0, i)),
            pl.BlockSpec((None, d, d), lambda c, i: (3, 0, 0)),
            per_chunk,
            per_chunk,
            pl.BlockSpec(vec.shape, lambda c, i: (0, 0)),
            pl.BlockSpec((None, 1, d), lambda c, i: (c, 0, 0)),
        ],
        out_specs=[
            pl.BlockSpec((d, tb), lambda c, i: (0, jnp.where(c == chunks - 1, i, 0))),
            pl.BlockSpec((None, d, tb), lambda c, i: (c, 0, i)),
            pl.BlockSpec((None, tb, lanes_of(d)), lambda c, i: (c, i, 0)),
            pl.BlockSpec((d, tb), first_t),
            pl.BlockSpec((d, tb), first_t),
            rows(final),
            rows(final),
            pl.BlockSpec((tb, lanes_of(d)), final),
            pl.BlockSpec((None, 1, d), lambda c, i: (c, 0, 0)),
            pl.BlockSpec((8, d), lambda c, i: (0, 0)),
        ],
        out_shape=[
            bft,
            jax.ShapeDtypeStruct((chunks, d, t), BF),
            jax.ShapeDtypeStruct((chunks, t, lanes_of(d)), BF),
            bft,
            bft,
            f32,
            bf,
            jax.ShapeDtypeStruct((t, lanes_of(d)), BF),
            jax.ShapeDtypeStruct((chunks, 1, d), F32),
            jax.ShapeDtypeStruct((8, d), F32),
        ],
        scratch_shapes=[
            pltpu.VMEM((t, d), F32),
            pltpu.VMEM((t, d), BF),
            pltpu.VMEM((t, d), F32),
            pltpu.VMEM((t, d), F32),
        ],
        compiler_params=params(2),
        name="mlp",
    )(x, mixed, cot, wa, wf, wp, vec, bfc)


def qkv_back_kernel(
    dq_ref, own_ref, next_ref, gb_ref, x_ref, ga_ref, wq_ref, wk_ref, wv_ref, vec_ref,
    dx_ref, gp_ref, sums_ref,
):
    @pl.when(pl.program_id(0) == 0)
    def _():
        sums_ref[...] = jnp.zeros_like(sums_ref)

    dq = dq_ref[...]
    width = dq.shape[1]
    dk = (own_ref[0] + next_ref[0, :, :width].astype(F32)).astype(BF)
    dv = (own_ref[1] + next_ref[1, :, :width].astype(F32)).astype(BF)
    gp_ref[0, :, :width] = dq
    gp_ref[1, :, :width] = dk
    gp_ref[2, :, :width] = dv
    gp_ref[3, :, :width] = gb_ref[...]
    grad = mm_nt(dq, wq_ref[...]) + mm_nt(dk, wk_ref[...]) + mm_nt(dv, wv_ref[...])
    normed, inv = standardize(x_ref[...].astype(F32).T)
    dx_ref[...] = (ga_ref[...] + norm_pullback(grad, normed, inv, vec_ref[0:1, :])).T
    sums_ref[0:1, :] += jnp.sum(dq.astype(F32), axis=0, keepdims=True)
    sums_ref[1:2, :] += jnp.sum(dv.astype(F32), axis=0, keepdims=True)
    sums_ref[2:3, :] += jnp.sum(grad * normed, axis=0, keepdims=True)
    sums_ref[3:4, :] += jnp.sum(grad, axis=0, keepdims=True)


def qkv_back(dq, own, nxt, gb, x, ga, wa, vec, tb):
    d, t = x.shape
    rows = pl.BlockSpec((tb, d), lambda i: (i, 0))
    turned = pl.BlockSpec((d, tb), lambda i: (0, i))
    pair = pl.BlockSpec((2, tb, d), lambda i: (0, i, 0))
    weight = lambda s: pl.BlockSpec((None, d, d), lambda i: (s, 0, 0))
    return pl.pallas_call(
        qkv_back_kernel,
        grid=(t // tb,),
        in_specs=[
            rows, pair, pl.BlockSpec((2, tb, lanes_of(d)), lambda i: (0, i, 0)), rows, turned, rows,
            weight(0), weight(1), weight(2),
            pl.BlockSpec(vec.shape, lambda i: (0, 0)),
        ],
        out_specs=[
            turned,
            pl.BlockSpec((4, tb, lanes_of(d)), lambda i: (0, i, 0)),
            pl.BlockSpec((8, d), lambda i: (0, 0)),
        ],
        out_shape=[
            jax.ShapeDtypeStruct((d, t), F32),
            jax.ShapeDtypeStruct((4, t, lanes_of(d)), BF),
            jax.ShapeDtypeStruct((8, d), F32),
        ],
        compiler_params=params(1),
        name="qkv_back",
    )(dq, own, nxt, gb, x, ga, wa, wa, wa, vec)


def weight_grad_kernel(turned, groups, extra, count, place_ref, *refs):
    operands, out_refs = refs[:count], refs[count:]
    extra_ref = operands[-1] if extra else None
    size, width = out_refs[0].shape[-2:]
    total = None
    for i in range(0, count - extra, 2):
        if turned:
            term = mm_nt(operands[i][...], operands[i + 1][...])
        else:
            term = mm(operands[i][...], operands[i + 1][:, :width])
        total = term if total is None else total + term
    total = total.astype(BF).reshape(groups, -1, width)
    for r, out_ref in enumerate(out_refs):

        @pl.when(pl.program_id(0) == r)
        def _():
            size = total.shape[1]
            out_ref[:, :size, :] = total
            if extra:
                out_ref[:, size:, :] = extra_ref[...]


def weight_grad(pairs, left_of, right_of, place, d, groups=1, turned=False, extra=None):
    m = pairs[0][0].shape[-2]
    specs, operands = [], []
    for left, right in pairs:
        specs.append(pl.BlockSpec((None,) + left.shape[1:], lambda r, s: (left_of(r, r ^ s[0]), 0, 0)))
        specs.append(pl.BlockSpec((None,) + right.shape[1:], lambda r, s: (right_of(r, r ^ s[0]), 0, 0)))
        operands += [left, right]
    size = m // groups
    if extra is not None:
        specs.append(pl.BlockSpec((None,) + extra.shape[1:], lambda r, s: (r, 0, 0, 0)))
        operands.append(extra)
        size += extra.shape[2]
    return pl.pallas_call(
        functools.partial(
            weight_grad_kernel, turned, groups, extra is not None, len(operands)
        ),
        grid_spec=pltpu.PrefetchScalarGridSpec(
            num_scalar_prefetch=1,
            grid=(4,),
            in_specs=specs,
            out_specs=[pl.BlockSpec((groups, size, d), lambda r, s: (0, 0, 0))] * 4,
        ),
        out_shape=[jax.ShapeDtypeStruct((groups, size, d), BF)] * 4,
        compiler_params=params(1),
        name="weight_grad",
    )(place, *operands)


def assemble_kernel(swapped, place_ref, own_ref, mine_ref, other_ref, out_ref, sems):
    chip, core, depth = place_ref[0], place_ref[1], place_ref[2]
    chunks, block, _ = own_ref.shape
    depths = mine_ref.shape[1] + 1
    piece = mine_ref.shape[2]
    skip = 2 * piece - block

    def target(chunk, z, start, size):
        row = pl.multiple_of((chunk if swapped else z) * block, 8) + start
        return out_ref.at[z if swapped else chunk, pl.ds(pl.multiple_of(row, 8), size), :]

    def run(halves):
        copies = []
        for r in range(chunks):
            chunk = r ^ chip
            copies.append((own_ref.at[chunk], target(chunk, depth, 0, block)))
            for d in range(1, depths):
                z = lax.rem(depth + d, depths)
                copies.append(
                    (halves[0].at[r, d - 1], target(chunk, z, 0, piece))
                )
                copies.append(
                    (
                        halves[1].at[r, d - 1, pl.ds(skip, piece - skip), :],
                        target(chunk, z, piece, piece - skip),
                    )
                )
        started = [
            pltpu.make_async_copy(source, there, sems.at[i])
            for i, (source, there) in enumerate(copies)
        ]
        for copy in started:
            copy.start()
        for copy in started:
            copy.wait()

    @pl.when(core == 0)
    def _():
        run((mine_ref, other_ref))

    @pl.when(core == 1)
    def _():
        run((other_ref, mine_ref))


def assemble(own, mine, other, place, swapped):
    chunks, block, width = own.shape
    depths = mine.shape[1] + 1
    shape = (depths, chunks * block, width) if swapped else (chunks, depths * block, width)
    hbm = pl.BlockSpec(memory_space=pl.ANY)
    return pl.pallas_call(
        functools.partial(assemble_kernel, swapped),
        in_specs=[pl.BlockSpec(memory_space=pltpu.SMEM), hbm, hbm, hbm],
        out_specs=pl.BlockSpec(memory_space=pltpu.VMEM),
        out_shape=jax.ShapeDtypeStruct(shape, own.dtype),
        scratch_shapes=[pltpu.SemaphoreType.DMA((chunks * (2 * depths - 1),))],
        compiler_params=pltpu.CompilerParams(vmem_limit_bytes=VMEM_LIMIT),
        name="assemble",
    )(place, own, mine, other)


def flip(value, bit):
    count = lax.axis_size("wide")
    return lax.ppermute(value, "wide", [(i, i ^ bit) for i in range(count)])


def along(value, distance):
    count = lax.axis_size("narrow")
    return lax.ppermute(value, "narrow", [(i, (i + distance) % count) for i in range(count)])


def from_behind(value, distance):
    count = lax.axis_size("narrow")
    route = [(i - distance, i) for i in range(count) if 0 <= i - distance < count]
    return lax.ppermute(value, "narrow", route)


def add_low(*terms):
    total = terms[0].astype(F32)
    for term in terms[1:]:
        total = total + term.astype(F32)
    return total.astype(BF)


def after(value, *others):
    return lax.optimization_barrier((value, others))[0]


def plane_near(value):
    return flip(value, 2), flip(value, 4)


def plane_far(near):
    across_x, across_y = near
    half = across_x.shape[-2] // 16 * 8
    return flip(across_x[..., :half, :], 4), flip(across_y[..., half:, :], 2)


def plane_all(value, near, far):
    return jnp.stack([value, *near, jnp.concatenate(far, axis=-2)])


def scatter_far(grads):
    half = grads[3].shape[-2] // 16 * 8
    return flip(grads[3][..., :half, :], 2), flip(grads[3][..., half:, :], 4)


def scatter_near(grads, far):
    upper, lower = far
    half = grads[3].shape[-2] // 16 * 8
    to_x = jnp.concatenate(
        [grads[1][..., :half, :], add_low(grads[1][..., half:, :], lower)], axis=-2
    )
    to_y = jnp.concatenate(
        [add_low(grads[2][..., :half, :], upper), grads[2][..., half:, :]], axis=-2
    )
    return to_x, to_y


def depth_scatter(grads):
    parts = [grads[0]]
    for d in range(1, grads.shape[0]):
        parts.append(along(grads[d], d))
    return add_low(*parts)


def roll_from(value, start, axis, count=None):
    count = count or value.shape[axis]
    twice = jnp.concatenate([value, lax.slice_in_dim(value, 0, count, axis=axis)], axis=axis)
    return lax.dynamic_slice_in_dim(twice, start, count, axis=axis)


def shards(
    inputs, cell_lengths, w_qkv, w_out, w_fc, w_proj, b_query, b_value, b_out, b_fc, b_proj,
    gain_attn, shift_attn, gain_mlp, shift_mlp, cotangent,
):
    _, span, d = inputs.shape
    depths = lax.axis_size("narrow")
    chips = lax.axis_size("wide") // 2
    block = w_qkv.shape[0]
    chunks = w_fc.shape[1] // d
    direct = chips == chunks == depths == 4 and block % 8 == 0
    wide_index = lax.axis_index("wide")
    chip, core = wide_index // 2, wide_index % 2
    depth = lax.axis_index("narrow")
    tb = min(256, span)
    qb = 128
    band = span + qb

    x_own = inputs.reshape(span, d).T
    cot = cotangent.reshape(span, d).T

    own_a = jnp.stack([w_qkv[:, i * d : (i + 1) * d] for i in range(3)] + [w_out])
    own_f = jnp.stack([w_fc[:, i * d : (i + 1) * d] for i in range(chunks)])
    small = jnp.concatenate(
        [b_query, b_value, b_out, b_proj, gain_attn, shift_attn, gain_mlp, shift_mlp, b_fc]
    ).reshape(1, -1)
    if direct:
        piece = -(-block // 16) * 8
        place = jnp.stack([chip, core, depth]).astype(jnp.int32)
        own_p = w_proj.reshape(chunks, block, d)

        def part(own):
            return lax.dynamic_slice(own, (chip, core * (block - piece), 0), (1, piece, d))[0]

        small_rows = small.shape[1] // d
        small = jnp.pad(small.reshape(small_rows, d), ((0, 8 - small_rows), (0, 0)))
        part_a = jnp.concatenate([part(own_a), small])
        part_f, part_p = part(own_f), part(own_p)
        arrived = [along(part_a, depths - e) for e in range(1, depths)]
        part_f, part_p = after((part_f, part_p), *arrived)
        x_prev = from_behind(x_own, 1)
        deep_f = lax.all_gather(part_f, "narrow", axis=0)
        deep_p = lax.all_gather(part_p, "narrow", axis=0)
        foreign = after(jnp.stack([a[:piece] for a in arrived]), x_prev)
        near = plane_near(foreign)
        mine = plane_all(foreign, near, plane_far(near))
        mine = after(mine, deep_f)
        other = flip(mine, 1)
        wa = assemble(own_a, mine, other, place, False)
        foreign_f = roll_from(after(deep_f, mine), (depth + 1) % depths, 0, depths - 1)
        near_f = plane_near(foreign_f)
        small = jnp.stack([part_a[piece:]] + [a[piece:] for a in arrived])
        small = roll_from(small, (depths - depth) % depths, 0)[:, :small_rows].reshape(depths, -1)
    else:
        everything = lambda value, axis: lax.all_gather(value, "narrow", axis=axis, tiled=True)
        x_prev = from_behind(x_own, 1)
        wa = everything(own_a, 1)
        wf = everything(own_f, 1)
        wp = everything(w_proj, 0).reshape(chunks, d, d)
        small = everything(small, 0)
    small = small.astype(F32)
    vectors = [small[:, i * block : (i + 1) * block].reshape(1, d) for i in range(8)]
    bias_q, bias_v, bias_o, bias_p, gain_1, shift_1, gain_2, shift_2 = vectors
    bias_f = small[:, 8 * block :].reshape(chunks, 1, d)
    vec_1 = jnp.concatenate([gain_1, shift_1, bias_q, bias_v] + [jnp.zeros_like(bias_q)] * 4)
    vec_2 = jnp.concatenate([bias_o, gain_2, shift_2, bias_p] + [jnp.zeros_like(bias_q)] * 4)

    starts = jnp.cumsum(cell_lengths, axis=-1) - cell_lengths
    pos = (depth - 1) * span + jnp.arange(2 * span, dtype=jnp.int32)
    ids = jnp.sum((starts <= pos[:, None]).astype(jnp.int32), axis=-1) - 1
    query_ids = ids[span:]
    first = ids[span::qb]
    reach = jnp.sum((ids[None, :] < first[:, None]).astype(jnp.int32), axis=-1) // qb
    need = jnp.arange(span // qb, dtype=jnp.int32) + (span // qb + 1) - reach
    key_ids = jnp.stack([ids[i * qb : i * qb + band] for i in range(span // qb)])

    q, k, v, nt_1 = ln_qkv(x_prev, x_own, wa, vec_1, tb)
    if direct:
        near_f, q = after((near_f, q), k)
        far_f = plane_far(near_f)
        foreign_p = roll_from(after(deep_p, *near_f), (depth + 1) % depths, 0, depths - 1)
        near_p = plane_near(foreign_p)
    mixed = attend(need, q, k, v, query_ids[:, None], key_ids[:, None, :], qb, d)
    if direct:
        far_f, near_p = after((far_f, near_p), mixed)
        far_p = plane_far(near_p)
        mine = plane_all(foreign_f, near_f, far_f)
        wf = assemble(own_f, mine, flip(mine, 1), place, False)
        mine = plane_all(foreign_p, near_p, far_p)
        wp = assemble(own_p, mine, flip(mine, 1), place, True)
    out, ht, gp_f, nt_2, mt, grad_after, grad_attn, grad_mixed, grad_bfc, sums_2 = mlp(
        x_own, mixed, cot, wa, wf, wp, vec_2, bias_f, tb
    )
    left_a = jnp.stack([nt_1, mt])
    if direct:
        def halves(value):
            take = lambda at: lax.dynamic_slice_in_dim(value, at * (block - piece), piece, axis=2)
            flat = lambda a: a.reshape(a.shape[0], depths * piece, span)
            return flat(take(core)), flip(flat(take(1 - core)), 1)

        def shard_of(mine, other):
            first = jnp.where(core == 0, mine, other)[:, :piece]
            second = jnp.where(core == 0, other, mine)[:, 2 * piece - block : piece, :]
            both = jnp.concatenate([first, second], axis=1)
            return [
                lax.dynamic_index_in_dim(both, i ^ chip, 0, keepdims=False).astype(F32)
                for i in range(chunks)
            ]

        by_chip = jnp.stack(
            [
                lax.dynamic_index_in_dim(
                    ht.reshape(depths, chunks, block, span), r ^ chip, 1, keepdims=False
                )
                for r in range(chunks)
            ]
        )
        here, there = halves(by_chip)
        cots = cot[None]
        grads_p = weight_grad(
            [(here, cots), (there, flip(cots, 1))],
            lambda r, c: r, lambda r, c: 0, place, d, depths, turned=True,
        )
        here_f, there_f = halves(nt_2.reshape(1, depths, block, span))
        gp_there = flip(gp_f, 1)
        grad_mixed = after(grad_mixed, *grads_p, there_f, gp_there)
        far_p = scatter_far(grads_p)

    dq, kv_prev, kv_own = attend_back(
        need, q, k, v, grad_mixed, query_ids[None, :], key_ids[:, :, None], qb, d
    )
    kv_next = from_behind(kv_prev, -1)
    if direct:
        to_x, to_y = scatter_near(grads_p, after(far_p, kv_prev))
        near_p = (flip(to_x, 2), flip(to_y, 4))
        grads_f = weight_grad(
            [(after(here_f, to_x, to_y), gp_f), (there_f, gp_there)],
            lambda r, c: 0, lambda r, c: c, place, d, depths,
        )
        far_f = scatter_far(grads_f)
        near_p = after(near_p, *grads_f)
        sum_p = add_low(grads_p[0], *near_p)
        to_x, to_y = scatter_near(grads_f, after(far_f, sum_p))
        near_f = (flip(to_x, 2), flip(to_y, 4))
        kv_next = after(kv_next, to_x, to_y)
    dx, gp_a, sums_1 = qkv_back(dq, kv_own, kv_next, grad_attn, x_own, grad_after, wa, vec_1, tb)

    rows = [sums_1[0], sums_1[1], sums_2[2], sums_2[3], sums_1[2], sums_1[3], sums_2[0], sums_2[1]]
    packed = jnp.concatenate(
        [r.reshape(depths, block) for r in rows] + [grad_bfc.reshape(depths, chunks * block)], axis=1
    )
    if direct:
        packed = packed + flip(packed, 1)
        packed = roll_from(packed, depth, 0).reshape(depths, chunks, -1)
        extra = jnp.stack(
            [lax.dynamic_index_in_dim(packed, r ^ chip, 1, keepdims=False) for r in range(chunks)]
        )[:, :, None, :]
        share = extra.shape[-1]
        extra = jnp.pad(extra, ((0, 0), (0, 0), (0, 7), (0, d - share))).astype(BF)
        sum_f = add_low(grads_f[0], *after(near_f, gp_a))
        gp_send = after(gp_a, sum_f)
        sum_p, sum_f = (
            lax.psum_scatter(v, "narrow", scatter_dimension=0, tiled=False) for v in (sum_p, sum_f)
        )
        here, there = halves(roll_from(left_a.reshape(2, depths, block, span), depth, 1))
        grads_a = weight_grad(
            [(here, gp_a), (there, flip(gp_send, 1))],
            lambda r, c: c // 3, lambda r, c: c, place, d, depths, extra=extra,
        )
        to_x, to_y = scatter_near(grads_a, scatter_far(grads_a))
        near_a = after((flip(to_x, 2), flip(to_y, 4)), sum_p, sum_f)
        sum_a = add_low(grads_a[0], *near_a)
        sum_pf = jnp.stack(after((sum_p, sum_f), sum_a))
        near_pf = plane_near(sum_pf)
        far_pf = plane_far(near_pf)
        mine_pf = plane_all(sum_pf, near_pf, far_pf)
        sum_a = after(depth_scatter(sum_a), *far_pf)
        near_a = plane_near(sum_a)
        mine = plane_all(sum_a, near_a, plane_far(near_a))
        other = flip(after(mine, mine_pf), 1)
        other_pf = flip(mine_pf, 1)
        shard_p = shard_of(mine_pf[:, 0], other_pf[:, 0])
        shard_f = shard_of(mine_pf[:, 1], other_pf[:, 1])
        shard_a = shard_of(mine, other)
        shard_p = jnp.concatenate(shard_p, axis=0)
        share_of = mine[:, piece, :share]
        packed = jnp.concatenate(
            [lax.dynamic_index_in_dim(share_of, i ^ chip, 0, keepdims=False) for i in range(chunks)]
        ).astype(F32)
    else:
        zero = jnp.zeros((1,), jnp.int32)

        def total(left, right, left_of, right_of, turned=False):
            grads = weight_grad([(left, right)], left_of, right_of, zero, d, turned=turned)
            return lax.psum(jnp.concatenate(grads).astype(F32), "wide")

        def reduce(grads, axis):
            return lax.psum_scatter(grads, "narrow", scatter_dimension=axis, tiled=True)

        shard_p = total(ht, cot[None], lambda r, c: c, lambda r, c: 0, True)
        shard_p = reduce(shard_p.reshape(chunks * d, d), 0)
        shard_f = reduce(total(nt_2[None], gp_f, lambda r, c: 0, lambda r, c: c), 1)
        shard_a = reduce(total(left_a, gp_a, lambda r, c: c // 3, lambda r, c: c), 1)
        packed = lax.psum(packed, ("wide", "narrow"))
        packed = lax.dynamic_index_in_dim(packed, depth, 0, keepdims=False)
    shard_qkv = jnp.concatenate([shard_a[i] for i in range(3)], axis=1)
    shard_fc = jnp.concatenate([shard_f[i] for i in range(chunks)], axis=1)

    small_grads = [packed[i * block : (i + 1) * block] for i in range(8)]
    g_bq, g_bv, g_bo, g_bp, g_g1, g_s1, g_g2, g_s2 = small_grads
    return (
        out.T.reshape(inputs.shape),
        dx.T.reshape(inputs.shape),
        shard_qkv,
        shard_a[3],
        shard_fc,
        shard_p,
        g_bq,
        g_bv,
        g_bo,
        packed[8 * block :],
        g_bp,
        g_g1,
        g_s1,
        g_g2,
        g_s2,
    )


def solution(mesh):
    rows, flat = P("narrow", None), P("narrow")
    tokens = P("wide", "narrow", None)
    in_specs = (tokens, P("wide", None)) + (rows,) * 4 + (flat,) * 9 + (tokens,)
    out_specs = (tokens, tokens) + (rows,) * 4 + (flat,) * 9
    return jax.shard_map(shards, mesh=mesh, in_specs=in_specs, out_specs=out_specs, check_vma=False)
```
